256 devices in a mesh: hist: 8 (over z), rows: 8 (over x_hi, y), dom: 4 (over x_lo, core).
Axes of the slice: x: 4 (x_hi: 2, x_lo: 2; x = x_hi * 2 + x_lo), y: 4, z: 8, core: 2. Of those that a mesh axis runs over, the one named last changes fastest.
Arguments:
- row_index: int32 [4, 262144], P(None, ('hist', 'rows', 'dom')), may hold values from 0 to 510
- col_index: int32 [4, 262144], P(None, ('hist', 'rows', 'dom')), may hold values from 0 to 510
- bin_index: int32 [4, 262144], P(None, ('hist', 'rows', 'dom')), may hold values from 0 to 255
- charge: bfloat16 [262144], P(('hist', 'rows', 'dom')), may hold values from 0.5 to 2
- momentum: float32 [2, 262144], P(None, ('hist', 'rows', 'dom')), may hold values from -6 to 6
- history: bfloat16 [64, 512, 512], P('hist', 'rows'), may hold values from 0 to 2
- kernel_cols: bfloat16 [64, 512, 512], P('hist', 'dom'), may hold values from -0.25 to 0.25
- kernel_rows: bfloat16 [64, 512, 2, 512], P('hist', 'rows'), may hold values from -0.03125 to 0.03125
Outputs:
- momentum_out: float32 [2, 262144], P(None, ('hist', 'rows', 'dom'))
- history_out: bfloat16 [64, 512, 512], P('hist', 'rows')
The draws below stay inside these ranges and needn't reach their ends.
All inputs are finite; a program needn't handle non-finite values.
Results may differ from the reference program's by a relative error of at most 0.0024.
Values may be sent and summed in bfloat16 or wider, within the bound.
No kernel may reach another device: no remote copies, remote signals or barrier semaphores. Data moves between devices by JAX's collectives and lax.ppermute only.
A program may use at most 64 MiB of HBM per device.

```python
import math
import jax
import jax.numpy as jnp
from jax import lax

NG = 512
BINS = 16
STEPS = 4
LAGS = 64
PARTICLES = 262144


def draw_row_index(key, part):
    shuffled = jax.random.permutation(jax.random.fold_in(key, 7), PARTICLES).astype(jnp.int32)
    centre = shuffled * (NG - 1) // PARTICLES
    drift_rows = jnp.arange(STEPS, dtype=jnp.int32)[:, None] - STEPS // 2
    jitter = jax.random.randint(jax.random.fold_in(key, 11), (STEPS, PARTICLES), -4, 5, dtype=jnp.int32)
    return jnp.clip(centre[None, :] + drift_rows + jitter, 0, NG - 2).astype(jnp.int32)


def set_ends(result, rng, smallest, high):
    extent = result.shape
    index_at = [jax.random.randint(jax.random.fold_in(rng, axis), (), 0, extent[axis]) for axis in range(len(extent))]
    result = result.at[tuple(index_at)].set(smallest)
    longest = extent.index(max(extent))
    index_at[longest] = (index_at[longest] + 1) % extent[longest]
    return result.at[tuple(index_at)].set(high)


def levels(key, dims, pieces, low, high):
    loudness, own = 1.0, jax.random.fold_in(key, 6)
    for position, blocks in pieces:
        draws = jnp.exp(jax.random.uniform(jax.random.fold_in(own, position), (blocks,), jnp.float32, low / len(pieces), high / len(pieces)))
        loudness = loudness * jnp.repeat(draws, dims[position] // blocks).reshape([-1 if axis == position else 1 for axis in range(len(dims))])
    return loudness


def noise(key, extent, deviation, limit, pieces=(), kind=jnp.bfloat16):
    drawn = jax.random.normal(key, extent, jnp.float32) * deviation
    if len(pieces) > 0:
        drawn = levels(key, extent, pieces, -0.22, 0.18) * drawn
    return jnp.clip(drawn, min=-limit, max=limit).astype(kind)


def setup_inputs(seed: int = 0) -> dict:
    arg_keys = jax.random.split(jax.random.key(seed), 9)
    row_index = draw_row_index(jax.random.fold_in(arg_keys[8], 71), 0)
    col_index = set_ends(jax.random.randint(arg_keys[1], (STEPS, PARTICLES), 0, NG - 1), jax.random.fold_in(arg_keys[1], 1), 0, (NG - 1) - 1).astype(jnp.int32)
    bin_index = set_ends(jax.random.randint(arg_keys[2], (STEPS, PARTICLES), 0, BINS * BINS), jax.random.fold_in(arg_keys[2], 1), 0, (BINS * BINS) - 1).astype(jnp.int32)
    charge = jnp.clip(jnp.exp(math.log(2.0) - 1.3862944 * jax.random.uniform(arg_keys[3], (PARTICLES,), jnp.float32) ** levels(arg_keys[3], (PARTICLES,), ((0, 256),), -0.2, 0.2)), 0.5, 2.0).astype(jnp.bfloat16)
    momentum = noise(arg_keys[4], (2, PARTICLES), 1.0, 6.0, ((1, 256),), jnp.float32)
    history = jnp.clip(2.0 * jax.random.uniform(arg_keys[5], (LAGS, NG, NG), jnp.float32) ** levels(arg_keys[5], (LAGS, NG, NG), ((0, 8), (1, 8)), -0.2, 0.2), 0.0, 2.0).astype(jnp.bfloat16)
    kernel_cols = noise(arg_keys[6], (LAGS, NG, NG), NG ** -0.5, 0.25, ((0, 8), (1, 4)))
    kernel_rows = noise(arg_keys[7], (LAGS, NG, 2, NG), (NG * LAGS) ** -0.5, 0.03125, ((0, 8), (1, 8)))
    return {"row_index": row_index, "col_index": col_index, "bin_index": bin_index, "charge": charge, "momentum": momentum, "history": history, "kernel_cols": kernel_cols, "kernel_rows": kernel_rows}


kick_scale = 0.5


def rounded(values):
    return lax.optimization_barrier(values.astype(jnp.bfloat16)).astype(jnp.float32)


def reference(row_index, col_index, bin_index, charge, momentum, history, kernel_cols, kernel_rows):
    charge_f = charge.astype(jnp.float32)
    cols_wide = kernel_cols.astype(jnp.float32)
    rows_wide = kernel_rows.astype(jnp.float32)
    cycle_now = history
    kick_sum = jnp.zeros((PARTICLES, 2), jnp.float32)
    for turn_index in range(STEPS):
        row_now = row_index[turn_index].astype(jnp.int32)
        col_now = col_index[turn_index].astype(jnp.int32)
        bin_now = bin_index[turn_index]
        frac_row = ((bin_now // BINS).astype(jnp.float32) + 0.5) / BINS
        frac_col = ((bin_now % BINS).astype(jnp.float32) + 0.5) / BINS
        lower = rounded(charge_f * (1.0 - frac_row))
        upper = rounded(charge_f * frac_row)
        density = jnp.zeros((NG, NG), jnp.float32)
        density = density.at[row_now, col_now].add(lower * (1.0 - frac_col))
        density = density.at[row_now, col_now + 1].add(lower * frac_col)
        density = density.at[row_now + 1, col_now].add(upper * (1.0 - frac_col))
        density = density.at[row_now + 1, col_now + 1].add(upper * frac_col)
        newest = density.astype(jnp.bfloat16)
        cycle_now = jnp.concatenate([newest[None], cycle_now[:-1]], axis=0)
        mixed_rows = jnp.einsum("kab,kjb->kaj", cycle_now.astype(jnp.float32), cols_wide).astype(jnp.bfloat16)
        field_full = rounded(jnp.einsum("kaci,kaj->icj", rows_wide, mixed_rows.astype(jnp.float32)))
        corner_aa = field_full[row_now, :, col_now]
        corner_ba = field_full[row_now + 1, :, col_now]
        corner_ab = field_full[row_now, :, col_now + 1]
        corner_bb = field_full[row_now + 1, :, col_now + 1]
        weight_row = frac_row[:, None]
        weight_col = frac_col[:, None]
        near_col = (1.0 - weight_row) * corner_aa + weight_row * corner_ba
        far_col = (1.0 - weight_row) * corner_ab + weight_row * corner_bb
        kick_sum = kick_sum + ((1.0 - weight_col) * near_col + weight_col * far_col)
    momentum_out = momentum + kick_scale * kick_sum.T
    return momentum_out, cycle_now
```

```python
import jax
import jax.numpy as jnp
from jax import lax
from jax.experimental import pallas as pl
from jax.experimental.pallas import tpu as pltpu
from jax.sharding import PartitionSpec as P

NG = 512
BINS = 16
STEPS = 4
LANES = 128

kick_scale = 0.5
f32 = jnp.float32
bf16 = jnp.bfloat16


def swap(array, axes):
    return lax.all_to_all(array, axes, split_axis=0, concat_axis=0, tiled=True)


def to_all(array, axes):
    copies = jnp.broadcast_to(array, (lax.axis_size(axes), *array.shape))
    return swap(copies, axes)


def hat(places, at):
    return jnp.maximum(1.0 - jnp.abs(places - at), 0.0)


def unpack(particles, source):
    lines = particles.shape[1] // 4

    def field(which):
        rows = [particles[source, which * lines + k : which * lines + k + 1, :] for k in range(lines)]
        return jnp.concatenate(rows, axis=1)

    bins = field(2)
    row_bin = jnp.floor(bins * (1.0 / BINS))
    col_bin = bins - row_bin * BINS
    at_row = field(0) + (row_bin + 0.5) * (1.0 / BINS)
    at_col = field(1) + (col_bin + 0.5) * (1.0 / BINS)
    return at_row, at_col, field(3)


def deposit_kernel(particles, out, total):
    source = pl.program_id(0)
    at_row, at_col, charge = unpack(particles, 0)
    places = lax.broadcasted_iota(jnp.int32, (NG, at_row.shape[1]), 0).astype(f32)
    row_table = (hat(places, at_row) * charge).astype(bf16)
    col_table = hat(places, at_col).astype(bf16)
    part = lax.dot_general(row_table, col_table, (((1,), (1,)), ((), ())), preferred_element_type=f32)

    @pl.when(source == 0)
    def _():
        total[...] = part

    @pl.when(source > 0)
    def _():
        total[...] += part

    @pl.when(source == pl.num_programs(0) - 1)
    def _():
        out[...] = total[...].reshape(out.shape).astype(bf16)


def deposit(particles, bands):
    sources, lines, _ = particles.shape
    return pl.pallas_call(
        deposit_kernel,
        grid=(sources,),
        in_specs=[pl.BlockSpec((1, lines, LANES), lambda i: (i, 0, 0))],
        out_specs=pl.BlockSpec((bands, NG // bands, NG), lambda i: (0, 0, 0)),
        out_shape=jax.ShapeDtypeStruct((bands, NG // bands, NG), bf16),
        scratch_shapes=[pltpu.VMEM((NG, NG), f32)],
        compiler_params=pltpu.CompilerParams(vmem_limit_bytes=48 << 20),
        name="deposit",
    )(particles)


def kick_kernel(particles, field, out):
    at_row, at_col, _ = unpack(particles, 0)
    shape = (NG, at_row.shape[1])
    places = lax.broadcasted_iota(jnp.int32, shape, 0)
    row_table = hat(places.astype(f32), at_row).astype(bf16)
    column = ((places >> 4) & 3) * 128 + (places >> 6) * 16 + (places & 15)
    col_table = hat(column.astype(f32), at_col)
    lines = shape[1] // LANES
    for comp in range(2):
        along = jnp.dot(field[:, comp * NG : (comp + 1) * NG], row_table, preferred_element_type=f32)
        kick = jnp.sum(along * col_table, axis=0, keepdims=True)
        for k in range(lines):
            out[0, comp * lines + k : comp * lines + k + 1, :] = kick[:, k * LANES : (k + 1) * LANES]


def kicks(particles, field):
    sources, lines, _ = particles.shape
    return pl.pallas_call(
        kick_kernel,
        grid=(sources,),
        in_specs=[
            pl.BlockSpec((1, lines, LANES), lambda i: (i, 0, 0)),
            pl.BlockSpec((NG, 2 * NG), lambda i: (0, 0)),
        ],
        out_specs=pl.BlockSpec((1, lines // 2, LANES), lambda i: (i, 0, 0)),
        out_shape=jax.ShapeDtypeStruct((sources, lines // 2, LANES), f32),
        compiler_params=pltpu.CompilerParams(vmem_limit_bytes=48 << 20),
        name="kicks",
    )(particles, field)


def old_mixed_kernel(history, cols, out):
    lags, band, _ = history.shape
    for lag in range(1, lags):
        steps = min(lag, STEPS)
        grids = history[lag - steps : lag].reshape(steps * band, NG)
        mixed = lax.dot_general(grids, cols[lag], (((1,), (1,)), ((), ())), preferred_element_type=f32)
        mixed = mixed.astype(bf16).reshape(steps, band, mixed.shape[1])
        for step in range(steps):
            out[step, lag] = mixed[steps - 1 - step]
    for step in range(STEPS):
        for lag in range(step + 1):
            out[step, lag] = jnp.zeros(out.shape[2:], bf16)


def old_mixed(history, cols):
    lags, band, _ = history.shape
    return pl.pallas_call(
        old_mixed_kernel,
        out_shape=jax.ShapeDtypeStruct((STEPS, lags, band, cols.shape[1]), bf16),
        compiler_params=pltpu.CompilerParams(vmem_limit_bytes=48 << 20),
        name="old_mixed",
    )(history, cols)


def field_kernel(first, fresh, incoming, cols, rows, mixed_old, out):
    band = incoming.shape[1]
    ahead = [jnp.where(first[0] == 1, fresh[STEPS - 1 - n], incoming[n]) for n in range(STEPS)]
    grids = jnp.concatenate(ahead, axis=0)
    wide = cols.shape[1]
    parts = [[] for _ in range(STEPS)]
    for lag in range(STEPS):
        count = STEPS - lag
        mixed = lax.dot_general(
            grids[lag * band :], cols[lag], (((1,), (1,)), ((), ())), preferred_element_type=f32
        ).astype(bf16)
        for n in range(count):
            parts[STEPS - 1 - n].append(mixed[n * band : (n + 1) * band])
    bands = out.shape[0] // STEPS
    share = wide // bands
    for step in range(STEPS):
        lines = parts[step] + [mixed_old[step, lag] for lag in range(step + 1, mixed_old.shape[1])]
        lhs = jnp.concatenate(lines, axis=0)
        field = lax.dot_general(lhs, rows[...], (((0,), (0,)), ((), ())), preferred_element_type=f32)
        field = field.astype(bf16)
        for band_to in range(bands):
            out[band_to * STEPS + step] = field[band_to * share : (band_to + 1) * share]


def field_parts(first, fresh, incoming, cols, rows, mixed_old, bands):
    wide = cols.shape[1]
    vmem = pl.BlockSpec(memory_space=pltpu.VMEM)
    return pl.pallas_call(
        field_kernel,
        in_specs=[pl.BlockSpec(memory_space=pltpu.SMEM)] + [vmem] * 5,
        out_specs=vmem,
        out_shape=jax.ShapeDtypeStruct((bands * STEPS, wide // bands, rows.shape[1]), bf16),
        compiler_params=pltpu.CompilerParams(vmem_limit_bytes=48 << 20),
        name="field_parts",
    )(first, fresh, incoming, cols, rows, mixed_old)


def local(row_index, col_index, bin_index, charge, momentum, history, kernel_cols, kernel_rows):
    lags, band, _ = history.shape
    count = charge.shape[0]
    bands = NG // band
    lines = count // LANES
    hist_at = lax.axis_index("hist")
    hist_size = lax.axis_size("hist")

    fields = [row_index.astype(f32), col_index.astype(f32), bin_index.astype(f32)]
    fields.append(jnp.broadcast_to(charge.astype(f32), (STEPS, count)))
    packed = jnp.stack([x.reshape(STEPS, lines, LANES) for x in fields], axis=1)
    particles = swap(packed.reshape(STEPS, 4 * lines, LANES), "dom")

    incoming = lax.ppermute(history[lags - STEPS :], "hist", [(i, i + 1) for i in range(hist_size - 1)])
    mixed_old = old_mixed(history, kernel_cols)
    rows_flat = kernel_rows.reshape(lags * band, 2 * NG)

    grid = deposit(particles, bands)
    by_band = jnp.sum(swap(grid, "rows").astype(f32), axis=0).astype(bf16)
    density = jnp.sum(to_all(by_band, "hist").astype(f32), axis=0).astype(bf16)
    fresh = to_all(density, "dom")

    first = (hist_at == 0).astype(jnp.int32).reshape(1)
    partial = field_parts(first, fresh, incoming, kernel_cols[:STEPS], rows_flat, mixed_old, bands)
    received = swap(partial, ("rows", "dom"))
    share = received.shape[1]
    by_column = jnp.sum(received.reshape(bands, STEPS * share, 2 * NG).astype(f32), axis=0).astype(bf16)
    summed = jnp.sum(to_all(by_column, "hist").astype(f32), axis=0).astype(bf16)
    field = to_all(summed, "rows").reshape(NG, 2 * NG)

    kick = swap(kicks(particles, field), "dom")
    kick_sum = jnp.sum(kick, axis=0).reshape(2, count)
    momentum_out = momentum + kick_scale * kick_sum

    ahead = jnp.where(hist_at == 0, fresh[::-1], incoming)
    history_out = jnp.concatenate([ahead, history[: lags - STEPS]], axis=0)
    return momentum_out, history_out


def solution(mesh):
    everyone = ("hist", "rows", "dom")
    in_specs = (
        P(None, everyone),
        P(None, everyone),
        P(None, everyone),
        P(everyone),
        P(None, everyone),
        P("hist", "rows", None),
        P("hist", "dom", None),
        P("hist", "rows", None, None),
    )
    out_specs = (P(None, everyone), P("hist", "rows", None))
    return jax.shard_map(local, mesh=mesh, in_specs=in_specs, out_specs=out_specs, check_vma=False)
```

```python
import functools

import jax
import jax.numpy as jnp
from jax import lax
from jax.experimental import pallas as pl
from jax.experimental.pallas import tpu as pltpu
from jax.sharding import PartitionSpec as P

NG = 512
BINS = 16
STEPS = 4
LANES = 128

kick_scale = 0.5
f32 = jnp.float32
bf16 = jnp.bfloat16


def swap(array, axes):
    return lax.all_to_all(array, axes, split_axis=0, concat_axis=0, tiled=True)


def to_all(array, axes):
    copies = jnp.broadcast_to(array, (lax.axis_size(axes), *array.shape))
    return swap(copies, axes)


def hat(places, cell, fraction):
    return jnp.maximum(1.0 - jnp.abs((places - cell) - fraction), jnp.zeros((), bf16))


def window(cell, first):
    return jnp.clip(cell - first, -2.0, 258.0).astype(bf16)


def unpack(particles, source):
    lines = particles.shape[1] // 4

    def field(which):
        rows = [particles[source, which * lines + k : which * lines + k + 1, :] for k in range(lines)]
        return jnp.concatenate(rows, axis=1)

    bins = field(2)
    row_bin = jnp.floor(bins * (1.0 / BINS))
    col_bin = bins - row_bin * BINS
    row_fraction = ((row_bin + 0.5) * (1.0 / BINS)).astype(bf16)
    col_fraction = ((col_bin + 0.5) * (1.0 / BINS)).astype(bf16)
    return field(0), row_fraction, field(1), col_fraction, field(3)


def lines_of(count, size):
    return lax.broadcasted_iota(jnp.int32, (count, size), 0)


def deposit_kernel(lines, band, parts, half, particles, out):
    sources, fields, _ = particles.shape
    bands, share = lines // band, band // parts
    places = lines_of(lines, fields // 4 * LANES).astype(f32).astype(bf16)
    total = None
    for source in range(sources):
        row, row_fraction, col, col_fraction, charge = unpack(particles, source)
        row_table = hat(places, window(row, (half[0] * lines).astype(f32)), row_fraction) * charge.astype(bf16)
        col_tables = [hat(places, window(col, float(first)), col_fraction) for first in range(0, NG, lines)]
        col_table = jnp.concatenate(col_tables, axis=0)
        part = lax.dot_general(row_table, col_table, (((1,), (1,)), ((), ())), preferred_element_type=f32)
        total = part if total is None else total + part
    grid = total.astype(bf16)
    for n in range(bands * parts):
        part, at = divmod(n, bands)
        first = at * band + part * share
        out[n] = grid[first : first + share]


def deposit(half, particles, lines, band, parts):
    blocks = (lines // band * parts, band // parts, NG)
    vmem = pl.BlockSpec(memory_space=pltpu.VMEM)
    return pl.pallas_call(
        functools.partial(deposit_kernel, lines, band, parts),
        in_specs=[pl.BlockSpec(memory_space=pltpu.SMEM), vmem],
        out_specs=vmem,
        out_shape=jax.ShapeDtypeStruct(blocks, bf16),
        compiler_params=pltpu.CompilerParams(vmem_limit_bytes=48 << 20),
        name="deposit",
    )(half, particles)


def kick_kernel(half, particles, field, out):
    sources, fields, _ = particles.shape
    width = field.shape[0]
    lines = fields // 4
    places = lines_of(width, lines * LANES)
    row_places = places.astype(f32).astype(bf16)
    column = (((places >> 4) & 3) * 128 + (places >> 6) * 16 + (places & 15)).astype(f32)

    def tables(source):
        row, row_fraction, col, col_fraction, _ = unpack(particles, source)
        row_tables = [hat(row_places, window(row, float(first)), row_fraction) for first in range(0, NG, width)]
        at_col = col + col_fraction.astype(f32) - (half[0] * 64).astype(f32)
        return jnp.concatenate(row_tables, axis=0), jnp.maximum(1.0 - jnp.abs(column - at_col), 0.0)

    ready = tables(0)
    for source in range(sources):
        row_table, col_table = ready
        if source + 1 < sources:
            ready = tables(source + 1)
        for comp in range(2):
            along = jnp.dot(field[:, comp * NG : (comp + 1) * NG], row_table, preferred_element_type=f32)
            kick = jnp.sum(along * col_table, axis=0, keepdims=True)
            for k in range(lines):
                out[source, comp * lines + k : comp * lines + k + 1, :] = kick[:, k * LANES : (k + 1) * LANES]


def kicks(half, particles, field):
    sources, fields, _ = particles.shape
    vmem = pl.BlockSpec(memory_space=pltpu.VMEM)
    return pl.pallas_call(
        kick_kernel,
        in_specs=[pl.BlockSpec(memory_space=pltpu.SMEM), vmem, vmem],
        out_specs=vmem,
        out_shape=jax.ShapeDtypeStruct((sources, fields // 2, LANES), f32),
        compiler_params=pltpu.CompilerParams(vmem_limit_bytes=48 << 20),
        name="kicks",
    )(half, particles, field)


def old_mixed_kernel(history, cols, out):
    lags, band, _ = history.shape
    for lag in range(1, lags):
        steps = min(lag, STEPS)
        grids = history[lag - steps : lag].reshape(steps * band, NG)
        mixed = lax.dot_general(grids, cols[lag], (((1,), (1,)), ((), ())), preferred_element_type=f32)
        mixed = mixed.astype(bf16).reshape(steps, band, mixed.shape[1])
        for step in range(steps):
            out[step, lag] = mixed[steps - 1 - step]
    for step in range(STEPS):
        for lag in range(step + 1):
            out[step, lag] = jnp.zeros(out.shape[2:], bf16)


def old_mixed(history, cols):
    lags, band, _ = history.shape
    return pl.pallas_call(
        old_mixed_kernel,
        out_shape=jax.ShapeDtypeStruct((STEPS, lags, band, cols.shape[1]), bf16),
        compiler_params=pltpu.CompilerParams(vmem_limit_bytes=48 << 20),
        name="old_mixed",
    )(history, cols)


def field_kernel(first, fresh, incoming, cols, rows, mixed_old, out, newer):
    band = incoming.shape[1]
    parts_in = fresh.shape[0] // STEPS
    ahead = []
    for n in range(STEPS):
        density = [fresh[part * STEPS + STEPS - 1 - n] for part in range(parts_in)]
        ahead.append(jnp.where(first[0] == 1, jnp.concatenate(density, axis=0), incoming[n]))
        newer[n] = ahead[n]
    grids = jnp.concatenate(ahead, axis=0)
    wide = cols.shape[1]
    parts = [[] for _ in range(STEPS)]
    for lag in range(STEPS):
        count = STEPS - lag
        mixed = lax.dot_general(
            grids[lag * band :], cols[lag], (((1,), (1,)), ((), ())), preferred_element_type=f32
        ).astype(bf16)
        for n in range(count):
            parts[STEPS - 1 - n].append(mixed[n * band : (n + 1) * band])
    bands = out.shape[0] // STEPS
    share = wide // bands
    for step in range(STEPS):
        lines = parts[step] + [mixed_old[step, lag] for lag in range(step + 1, mixed_old.shape[1])]
        lhs = jnp.concatenate(lines, axis=0)
        field = lax.dot_general(lhs, rows[...], (((0,), (0,)), ((), ())), preferred_element_type=f32)
        field = field.astype(bf16)
        for band_to in range(bands):
            out[band_to * STEPS + step] = field[band_to * share : (band_to + 1) * share]


def field_parts(first, fresh, incoming, cols, rows, mixed_old, bands):
    wide = cols.shape[1]
    vmem = pl.BlockSpec(memory_space=pltpu.VMEM)
    return pl.pallas_call(
        field_kernel,
        in_specs=[pl.BlockSpec(memory_space=pltpu.SMEM)] + [vmem] * 5,
        out_specs=(vmem, vmem),
        out_shape=(
            jax.ShapeDtypeStruct((bands * STEPS, wide // bands, rows.shape[1]), bf16),
            jax.ShapeDtypeStruct(incoming.shape, bf16),
        ),
        compiler_params=pltpu.CompilerParams(vmem_limit_bytes=48 << 20),
        name="field_parts",
    )(first, fresh, incoming, cols, rows, mixed_old)


def local(row_index, col_index, bin_index, charge, momentum, history, kernel_cols, kernel_rows):
    lags, band, _ = history.shape
    count = charge.shape[0]
    bands = NG // band
    lines = count // LANES
    hist_at = lax.axis_index("hist")
    hist_size = lax.axis_size("hist")

    fields = [row_index.astype(f32), col_index.astype(f32), bin_index.astype(f32)]
    fields.append(jnp.broadcast_to(charge.astype(f32), (STEPS, count)))
    packed = jnp.stack([x.reshape(STEPS, lines, LANES) for x in fields], axis=1)
    packed = jnp.broadcast_to(packed.reshape(STEPS, 4 * lines, LANES), (2, STEPS, 4 * lines, LANES))
    particles = swap(packed.reshape(2 * STEPS, 4 * lines, LANES), ("xh", "dom"))
    half = lax.axis_index("xh").reshape(1)

    incoming = lax.ppermute(history[lags - STEPS :], "hist", [(i, i + 1) for i in range(hist_size - 1)])
    mixed_old = old_mixed(history, kernel_cols)
    rows_flat = kernel_rows.reshape(lags * band, 2 * NG)

    grid = deposit(half, particles, NG // 2, band, hist_size)
    grid, incoming = lax.optimization_barrier((grid, incoming))
    density = jnp.sum(swap(grid, ("hist", "y")).astype(f32), axis=0).astype(bf16)
    fresh = to_all(density, ("hist", "dom"))

    first = (hist_at == 0).astype(jnp.int32).reshape(1)
    partial, ahead = field_parts(first, fresh, incoming, kernel_cols[:STEPS], rows_flat, mixed_old, bands)
    received = swap(partial, ("xh", "y", "dom"))
    share = received.shape[1]
    by_column = jnp.sum(received.reshape(bands, STEPS * share, 2 * NG).astype(f32), axis=0)
    by_column = by_column.reshape(hist_size, -1, 2 * NG)
    summed = jnp.sum(swap(by_column, "hist"), axis=0).astype(bf16)
    whole = to_all(summed, "hist").reshape(STEPS * share, 2 * NG)
    field = to_all(whole, "y").reshape(NG // 2, 2 * NG)

    kick = swap(kicks(half, particles, field), ("xh", "dom"))
    kick_sum = jnp.sum(kick, axis=0).reshape(2, count)
    momentum_out = momentum + kick_scale * kick_sum

    history_out = jnp.concatenate([ahead, history[: lags - STEPS]], axis=0)
    return momentum_out, history_out


def solution(mesh):
    split = {"hist": ("hist",), "rows": ("xh", "y"), "dom": ("dom",)}
    sizes = [mesh.shape["hist"], 2, mesh.shape["rows"] // 2, mesh.shape["dom"]]
    fine = jax.sharding.Mesh(mesh.devices.reshape(sizes), ("hist", "xh", "y", "dom"))

    def spec(*dims):
        return P(*[None if dim is None else tuple(a for name in dim for a in split[name]) for dim in dims])

    everyone = ("hist", "rows", "dom")
    in_specs = (
        spec(None, everyone),
        spec(None, everyone),
        spec(None, everyone),
        spec(everyone),
        spec(None, everyone),
        spec(["hist"], ["rows"], None),
        spec(["hist"], ["dom"], None),
        spec(["hist"], ["rows"], None, None),
    )
    out_specs = (spec(None, everyone), spec(["hist"], ["rows"], None))
    return jax.shard_map(local, mesh=fine, in_specs=in_specs, out_specs=out_specs, check_vma=False)
```

```python
import functools

import jax
import jax.numpy as jnp
from jax import lax
from jax.experimental import pallas as pl
from jax.experimental.pallas import tpu as pltpu
from jax.sharding import PartitionSpec as P

NG = 512
BINS = 16
STEPS = 4
LANES = 128

kick_scale = 0.5
f32 = jnp.float32
bf16 = jnp.bfloat16


def swap(array, axes):
    return lax.all_to_all(array, axes, split_axis=0, concat_axis=0, tiled=True)


def to_all(array, axes):
    copies = jnp.broadcast_to(array, (lax.axis_size(axes), *array.shape))
    return swap(copies, axes)


def hat(places, cell, fraction):
    return jnp.maximum(1.0 - jnp.abs((places - cell) - fraction), jnp.zeros((), bf16))


def window(cell, first):
    return jnp.clip(cell - first, -2.0, 258.0).astype(bf16)


def unpack(particles, source):
    def field(which):
        return particles[source, which : which + 1, :]

    bins = field(2)
    row_bin = jnp.floor(bins * (1.0 / BINS))
    col_bin = bins - row_bin * BINS
    row_fraction = ((row_bin + 0.5) * (1.0 / BINS)).astype(bf16)
    col_fraction = ((col_bin + 0.5) * (1.0 / BINS)).astype(bf16)
    return field(0), row_fraction, field(1), col_fraction, field(3)


def lines_of(count, size):
    return lax.broadcasted_iota(jnp.int32, (count, size), 0)


def pack_kernel(row, col, bins, charge, out):
    steps, count = row.shape
    weight = charge[...].astype(f32).reshape(1, count)
    halves = out.shape[0] // steps
    for step in range(steps):
        fields = [ref[step : step + 1, :].astype(f32) for ref in (row, col, bins)]
        packed = jnp.concatenate(fields + [weight], axis=0)
        for half in range(halves):
            out[step * halves + half] = packed


def pack(row, col, bins, charge, halves):
    steps, count = row.shape
    vmem = pl.BlockSpec(memory_space=pltpu.VMEM)
    return pl.pallas_call(
        pack_kernel,
        in_specs=[vmem] * 4,
        out_specs=vmem,
        out_shape=jax.ShapeDtypeStruct((halves * steps, 4, count), f32),
        name="pack",
    )(row, col, bins, charge)


def deposit_kernel(lines, band, parts, half, particles, out):
    sources, _, count = particles.shape
    bands, share = lines // band, band // parts
    places = lines_of(lines, count).astype(f32).astype(bf16)
    total = None
    for source in range(sources):
        row, row_fraction, col, col_fraction, charge = unpack(particles, source)
        row_table = hat(places, window(row, (half[0] * lines).astype(f32)), row_fraction) * charge.astype(bf16)
        col_tables = [hat(places, window(col, float(first)), col_fraction) for first in range(0, NG, lines)]
        col_table = jnp.concatenate(col_tables, axis=0)
        part = lax.dot_general(row_table, col_table, (((1,), (1,)), ((), ())), preferred_element_type=f32)
        total = part if total is None else total + part
    grid = total.astype(bf16)
    for n in range(bands * parts):
        at, part = divmod(n, parts)
        first = at * band + part * share
        out[n] = grid[first : first + share]


def deposit(half, particles, lines, band, parts):
    blocks = (lines // band * parts, band // parts, NG)
    vmem = pl.BlockSpec(memory_space=pltpu.VMEM)
    return pl.pallas_call(
        functools.partial(deposit_kernel, lines, band, parts),
        in_specs=[pl.BlockSpec(memory_space=pltpu.SMEM), vmem],
        out_specs=vmem,
        out_shape=jax.ShapeDtypeStruct(blocks, bf16),
        compiler_params=pltpu.CompilerParams(vmem_limit_bytes=48 << 20),
        cost_estimate=pl.CostEstimate(flops=4 * NG * NG * 4096, transcendentals=0, bytes_accessed=1 << 20),
        name="deposit",
    )(half, particles)


def kick_kernel(half, particles, field, out):
    sources, _, count = particles.shape
    width = field.shape[0]
    lines = count // LANES
    places = lines_of(width, count)
    row_places = places.astype(f32).astype(bf16)
    column = ((places >> 4) & 3) * 128 + (places >> 6) * 16 + (places & 15)
    column = column.astype(f32)

    def tables(source):
        row, row_fraction, col, col_fraction, _ = unpack(particles, source)
        row_tables = [hat(row_places, window(row, float(first)), row_fraction) for first in range(0, NG, width)]
        at_col = col + col_fraction.astype(f32) - (half[0] * 64).astype(f32)
        return jnp.concatenate(row_tables, axis=0), jnp.maximum(1.0 - jnp.abs(column - at_col), 0.0)

    ready = tables(0)
    for source in range(sources):
        row_table, col_table = ready
        if source + 1 < sources:
            ready = tables(source + 1)
        for comp in range(2):
            along = jnp.dot(field[:, comp * NG : (comp + 1) * NG], row_table, preferred_element_type=f32)
            kick = jnp.sum(along * col_table, axis=0, keepdims=True)
            for k in range(lines):
                out[source, comp * lines + k : comp * lines + k + 1, :] = kick[:, k * LANES : (k + 1) * LANES]


def kicks(half, particles, field):
    sources, _, count = particles.shape
    vmem = pl.BlockSpec(memory_space=pltpu.VMEM)
    return pl.pallas_call(
        kick_kernel,
        in_specs=[pl.BlockSpec(memory_space=pltpu.SMEM), vmem, vmem],
        out_specs=vmem,
        out_shape=jax.ShapeDtypeStruct((sources, 2 * count // LANES, LANES), f32),
        compiler_params=pltpu.CompilerParams(vmem_limit_bytes=48 << 20),
        name="kicks",
    )(half, particles, field)


def old_mixed_kernel(history, cols, out, kept):
    lags, band, _ = history.shape
    for lag in range(1, lags):
        steps = min(lag, STEPS)
        grids = history[lag - steps : lag].reshape(steps * band, NG)
        mixed = lax.dot_general(grids, cols[lag], (((1,), (1,)), ((), ())), preferred_element_type=f32)
        mixed = mixed.astype(bf16).reshape(steps, band, mixed.shape[1])
        for step in range(steps):
            out[step, lag] = mixed[steps - 1 - step]
    for step in range(STEPS):
        for lag in range(step + 1):
            out[step, lag] = jnp.zeros(out.shape[2:], bf16)
    kept[...] = history[: lags - STEPS]


def old_mixed(history, cols):
    lags, band, _ = history.shape
    return pl.pallas_call(
        old_mixed_kernel,
        out_shape=(
            jax.ShapeDtypeStruct((STEPS, lags, band, cols.shape[1]), bf16),
            jax.ShapeDtypeStruct((lags - STEPS, *history.shape[1:]), bf16),
        ),
        compiler_params=pltpu.CompilerParams(vmem_limit_bytes=48 << 20),
        name="old_mixed",
    )(history, cols)


def field_kernel(first, core, fresh, mine, other, cols, rows, mixed_old, out, newer):
    band = mine.shape[1]
    parts_in = fresh.shape[0] // STEPS
    ahead = []
    for n in range(STEPS):
        density = [fresh[(STEPS - 1 - n) * parts_in + part] for part in range(parts_in)]
        older = jnp.where(core[0] == n // 2, mine[n % 2], other[n % 2])
        ahead.append(jnp.where(first[0] == 1, jnp.concatenate(density, axis=0), older))
        newer[n] = ahead[n]
    grids = jnp.concatenate(ahead, axis=0)
    wide = cols.shape[1]
    parts = [[] for _ in range(STEPS)]
    for lag in range(STEPS):
        count = STEPS - lag
        mixed = lax.dot_general(
            grids[lag * band :], cols[lag], (((1,), (1,)), ((), ())), preferred_element_type=f32
        ).astype(bf16)
        for n in range(count):
            parts[STEPS - 1 - n].append(mixed[n * band : (n + 1) * band])
    bands = out.shape[0] // STEPS
    share = wide // bands
    for step in range(STEPS):
        lines = parts[step] + [mixed_old[step, lag] for lag in range(step + 1, mixed_old.shape[1])]
        lhs = jnp.concatenate(lines, axis=0)
        field = lax.dot_general(lhs, rows[...], (((0,), (0,)), ((), ())), preferred_element_type=f32)
        field = field.astype(bf16)
        for band_to in range(bands):
            half, quarter = divmod(band_to, bands // 2)
            out[(quarter * STEPS + step) * 2 + half] = field[band_to * share : (band_to + 1) * share]


def field_parts(place, fresh, mine, other, cols, rows, mixed_old, bands):
    wide = cols.shape[1]
    vmem = pl.BlockSpec(memory_space=pltpu.VMEM)
    return pl.pallas_call(
        field_kernel,
        in_specs=[pl.BlockSpec(memory_space=pltpu.SMEM)] * 2 + [vmem] * 6,
        out_specs=(vmem, vmem),
        out_shape=(
            jax.ShapeDtypeStruct((bands * STEPS, wide // bands, rows.shape[1]), bf16),
            jax.ShapeDtypeStruct((STEPS, *mine.shape[1:]), bf16),
        ),
        compiler_params=pltpu.CompilerParams(vmem_limit_bytes=48 << 20),
        name="field_parts",
    )(*place, fresh, mine, other, cols, rows, mixed_old)


def local(row_index, col_index, bin_index, charge, momentum, history, kernel_cols, kernel_rows):
    lags, band, _ = history.shape
    count = charge.shape[0]
    bands = NG // band
    hist_at = lax.axis_index("hist")
    hist_size = lax.axis_size("hist")

    particles = swap(pack(row_index, col_index, bin_index, charge, 2), ("dom", "xh"))
    core = lax.axis_index("dom") % 2
    half = lax.axis_index("xh").reshape(1)
    place = [(hist_at == 0).astype(jnp.int32).reshape(1), core.reshape(1)]

    mixed_old, kept = old_mixed(history, kernel_cols)
    tail = lax.dynamic_slice_in_dim(history, lags - STEPS + 2 * core, 2, 0)
    mine = lax.ppermute(tail, "hist", [(i, i + 1) for i in range(hist_size - 1)])
    rows_flat = kernel_rows.reshape(lags * band, 2 * NG)

    grid = deposit(half, particles, NG // 2, band, hist_size)
    grid, mine = lax.optimization_barrier((grid, mine))
    other = lax.ppermute(mine, "dom", [(i, i ^ 1) for i in range(STEPS)])
    density = jnp.sum(swap(grid, ("y", "hist")).astype(f32), axis=0).astype(bf16)
    fresh = to_all(density, ("dom", "hist"))

    partial, ahead = field_parts(place, fresh, mine, other, kernel_cols[:STEPS], rows_flat, mixed_old, bands)
    received = swap(partial, ("y", "dom", "xh"))
    share = received.shape[1]
    by_column = jnp.sum(received.reshape(bands // 2, STEPS, 2, share, 2 * NG).astype(f32), axis=(0, 2))
    by_column = by_column.reshape(hist_size, -1, 2 * NG)
    summed = jnp.sum(swap(by_column, "hist"), axis=0).astype(bf16)
    field = to_all(summed, ("y", "hist")).reshape(NG // 2, 2 * NG)

    kick = swap(kicks(half, particles, field), ("dom", "xh"))
    kick_sum = jnp.sum(kick, axis=0).reshape(2, count)
    momentum_out = momentum + kick_scale * kick_sum

    history_out = jnp.concatenate([ahead, kept], axis=0)
    return momentum_out, history_out


def solution(mesh):
    split = {"hist": ("hist",), "rows": ("xh", "y"), "dom": ("dom",)}
    sizes = [mesh.shape["hist"], 2, mesh.shape["rows"] // 2, mesh.shape["dom"]]
    fine = jax.sharding.Mesh(mesh.devices.reshape(sizes), ("hist", "xh", "y", "dom"))

    def spec(*dims):
        return P(*[None if dim is None else tuple(a for name in dim for a in split[name]) for dim in dims])

    everyone = ("hist", "rows", "dom")
    in_specs = (
        spec(None, everyone),
        spec(None, everyone),
        spec(None, everyone),
        spec(everyone),
        spec(None, everyone),
        spec(["hist"], ["rows"], None),
        spec(["hist"], ["dom"], None),
        spec(["hist"], ["rows"], None, None),
    )
    out_specs = (spec(None, everyone), spec(["hist"], ["rows"], None))
    return jax.shard_map(local, mesh=fine, in_specs=in_specs, out_specs=out_specs, check_vma=False)
```

```python
import functools

import jax
import jax.numpy as jnp
from jax import lax
from jax.experimental import pallas as pl
from jax.experimental.pallas import tpu as pltpu
from jax.sharding import PartitionSpec as P

NG = 512
BINS = 16
STEPS = 4
LANES = 128

kick_scale = 0.5
f32 = jnp.float32
bf16 = jnp.bfloat16


def swap(array, axes):
    return lax.all_to_all(array, axes, split_axis=0, concat_axis=0, tiled=True)


def to_all(array, axes):
    copies = jnp.broadcast_to(array, (lax.axis_size(axes), *array.shape))
    return swap(copies, axes)


def hat(places, cell, fraction):
    return jnp.maximum(1.0 - jnp.abs((places - cell) - fraction), jnp.zeros((), bf16))


def window(cell, first):
    return jnp.clip(cell - first, -2.0, 258.0).astype(bf16)


def unpack(particles, source):
    def field(which):
        return particles[source, which : which + 1, :]

    bins = field(2)
    row_bin = jnp.floor(bins * (1.0 / BINS))
    col_bin = bins - row_bin * BINS
    row_fraction = ((row_bin + 0.5) * (1.0 / BINS)).astype(bf16)
    col_fraction = ((col_bin + 0.5) * (1.0 / BINS)).astype(bf16)
    return field(0), row_fraction, field(1), col_fraction, field(3)


def lines_of(count, size):
    return lax.broadcasted_iota(jnp.int32, (count, size), 0)


def pack_kernel(row, col, bins, charge, out):
    steps, count = row.shape
    weight = charge[...].astype(f32).reshape(1, count)
    halves = out.shape[0] // steps
    for step in range(steps):
        fields = [ref[step : step + 1, :].astype(f32) for ref in (row, col, bins)]
        packed = jnp.concatenate(fields + [weight], axis=0)
        for half in range(halves):
            out[step * halves + half] = packed


def pack(row, col, bins, charge, halves):
    steps, count = row.shape
    vmem = pl.BlockSpec(memory_space=pltpu.VMEM)
    return pl.pallas_call(
        pack_kernel,
        in_specs=[vmem] * 4,
        out_specs=vmem,
        out_shape=jax.ShapeDtypeStruct((halves * steps, 4, count), f32),
        name="pack",
    )(row, col, bins, charge)


def deposit_kernel(lines, band, parts, half, particles, out):
    sources, _, count = particles.shape
    bands, share = lines // band, band // parts
    places = lines_of(lines, count).astype(f32).astype(bf16)
    total = None
    for source in range(sources):
        row, row_fraction, col, col_fraction, charge = unpack(particles, source)
        row_table = hat(places, window(row, (half[0] * lines).astype(f32)), row_fraction) * charge.astype(bf16)
        col_tables = [hat(places, window(col, float(first)), col_fraction) for first in range(0, NG, lines)]
        col_table = jnp.concatenate(col_tables, axis=0)
        part = lax.dot_general(row_table, col_table, (((1,), (1,)), ((), ())), preferred_element_type=f32)
        total = part if total is None else total + part
    grid = total.astype(bf16)
    for n in range(bands * parts):
        at, part = divmod(n, parts)
        first = at * band + part * share
        out[n] = grid[first : first + share]


def deposit(half, particles, lines, band, parts):
    blocks = (lines // band * parts, band // parts, NG)
    vmem = pl.BlockSpec(memory_space=pltpu.VMEM)
    return pl.pallas_call(
        functools.partial(deposit_kernel, lines, band, parts),
        in_specs=[pl.BlockSpec(memory_space=pltpu.SMEM), vmem],
        out_specs=vmem,
        out_shape=jax.ShapeDtypeStruct(blocks, bf16),
        compiler_params=pltpu.CompilerParams(vmem_limit_bytes=48 << 20),
        cost_estimate=pl.CostEstimate(flops=4 * NG * NG * 4096, transcendentals=0, bytes_accessed=1 << 20),
        name="deposit",
    )(half, particles)


def kick_kernel(half, particles, field, out):
    sources, _, count = particles.shape
    width = field.shape[0]
    lines = count // LANES
    places = lines_of(width, count)
    row_places = places.astype(f32).astype(bf16)
    column = ((places >> 4) & 3) * 128 + (places >> 6) * 16 + (places & 15)
    column = column.astype(f32)

    def tables(source):
        row, row_fraction, col, col_fraction, _ = unpack(particles, source)
        row_tables = [hat(row_places, window(row, float(first)), row_fraction) for first in range(0, NG, width)]
        at_col = col + col_fraction.astype(f32) - (half[0] * 64).astype(f32)
        return jnp.concatenate(row_tables, axis=0), jnp.maximum(1.0 - jnp.abs(column - at_col), 0.0)

    ready = tables(0)
    for source in range(sources):
        row_table, col_table = ready
        if source + 1 < sources:
            ready = tables(source + 1)
        for comp in range(2):
            along = jnp.dot(field[:, comp * NG : (comp + 1) * NG], row_table, preferred_element_type=f32)
            kick = jnp.sum(along * col_table, axis=0, keepdims=True)
            for k in range(lines):
                out[source, comp * lines + k : comp * lines + k + 1, :] = kick[:, k * LANES : (k + 1) * LANES]


def kicks(half, particles, field):
    sources, _, count = particles.shape
    vmem = pl.BlockSpec(memory_space=pltpu.VMEM)
    return pl.pallas_call(
        kick_kernel,
        in_specs=[pl.BlockSpec(memory_space=pltpu.SMEM), vmem, vmem],
        out_specs=vmem,
        out_shape=jax.ShapeDtypeStruct((sources, 2 * count // LANES, LANES), f32),
        compiler_params=pltpu.CompilerParams(vmem_limit_bytes=48 << 20),
        name="kicks",
    )(half, particles, field)


def old_mixed_kernel(history, cols, out, kept):
    lags, band, _ = history.shape
    for lag in range(1, lags):
        steps = min(lag, STEPS)
        grids = history[lag - steps : lag].reshape(steps * band, NG)
        mixed = lax.dot_general(grids, cols[lag], (((1,), (1,)), ((), ())), preferred_element_type=f32)
        mixed = mixed.astype(bf16).reshape(steps, band, mixed.shape[1])
        for step in range(steps):
            out[step, lag] = mixed[steps - 1 - step]
    for step in range(STEPS):
        for lag in range(step + 1):
            out[step, lag] = jnp.zeros(out.shape[2:], bf16)
    kept[STEPS:] = history[: lags - STEPS]


def old_mixed(history, cols):
    lags, band, _ = history.shape
    return pl.pallas_call(
        old_mixed_kernel,
        out_shape=(
            jax.ShapeDtypeStruct((STEPS, lags, band, cols.shape[1]), bf16),
            jax.ShapeDtypeStruct(history.shape, bf16),
        ),
        compiler_params=pltpu.CompilerParams(vmem_limit_bytes=48 << 20),
        name="old_mixed",
    )(history, cols)


def field_kernel(first, core, fresh, mine, other, cols, rows, mixed_old, kept, out, cycle, newer, sem):
    band = mine.shape[1]
    parts_in = fresh.shape[0] // STEPS
    ahead = []
    for n in range(STEPS):
        density = [fresh[(STEPS - 1 - n) * parts_in + part] for part in range(parts_in)]
        older = jnp.where(core[0] == n // 2, mine[n % 2], other[n % 2])
        ahead.append(jnp.where(first[0] == 1, jnp.concatenate(density, axis=0), older))
        newer[n] = ahead[n]
    store = pltpu.make_async_copy(newer, cycle.at[pl.ds(0, STEPS)], sem)
    store.start()
    grids = jnp.concatenate(ahead, axis=0)
    wide = cols.shape[1]
    parts = [[] for _ in range(STEPS)]
    for lag in range(STEPS):
        count = STEPS - lag
        mixed = lax.dot_general(
            grids[lag * band :], cols[lag], (((1,), (1,)), ((), ())), preferred_element_type=f32
        ).astype(bf16)
        for n in range(count):
            parts[STEPS - 1 - n].append(mixed[n * band : (n + 1) * band])
    bands = out.shape[0] // STEPS
    share = wide // bands
    for step in range(STEPS):
        lines = parts[step] + [mixed_old[step, lag] for lag in range(step + 1, mixed_old.shape[1])]
        lhs = jnp.concatenate(lines, axis=0)
        field = lax.dot_general(lhs, rows[...], (((0,), (0,)), ((), ())), preferred_element_type=f32)
        field = field.astype(bf16)
        for band_to in range(bands):
            half, quarter = divmod(band_to, bands // 2)
            out[(quarter * STEPS + step) * 2 + half] = field[band_to * share : (band_to + 1) * share]
    store.wait()


def field_parts(place, fresh, mine, other, cols, rows, mixed_old, kept, bands):
    wide = cols.shape[1]
    vmem = pl.BlockSpec(memory_space=pltpu.VMEM)
    return pl.pallas_call(
        field_kernel,
        in_specs=[pl.BlockSpec(memory_space=pltpu.SMEM)] * 2 + [vmem] * 6 + [pl.BlockSpec(memory_space=pl.ANY)],
        out_specs=(vmem, pl.BlockSpec(memory_space=pl.ANY)),
        out_shape=(
            jax.ShapeDtypeStruct((bands * STEPS, wide // bands, rows.shape[1]), bf16),
            jax.ShapeDtypeStruct(kept.shape, bf16),
        ),
        scratch_shapes=[pltpu.VMEM((STEPS, *mine.shape[1:]), bf16), pltpu.SemaphoreType.DMA],
        input_output_aliases={8: 1},
        compiler_params=pltpu.CompilerParams(vmem_limit_bytes=48 << 20),
        name="field_parts",
    )(*place, fresh, mine, other, cols, rows, mixed_old, kept)


def local(row_index, col_index, bin_index, charge, momentum, history, kernel_cols, kernel_rows):
    lags, band, _ = history.shape
    count = charge.shape[0]
    bands = NG // band
    hist_at = lax.axis_index("hist")
    hist_size = lax.axis_size("hist")

    particles = swap(pack(row_index, col_index, bin_index, charge, 2), ("dom", "xh"))
    core = lax.axis_index("dom") % 2
    half = lax.axis_index("xh").reshape(1)
    place = [(hist_at == 0).astype(jnp.int32).reshape(1), core.reshape(1)]

    mixed_old, kept = old_mixed(history, kernel_cols)
    tail = lax.dynamic_slice_in_dim(history, lags - STEPS + 2 * core, 2, 0)
    mine = lax.ppermute(tail, "hist", [(i, i + 1) for i in range(hist_size - 1)])
    rows_flat = kernel_rows.reshape(lags * band, 2 * NG)

    grid = deposit(half, particles, NG // 2, band, hist_size)
    grid, mine = lax.optimization_barrier((grid, mine))
    other = lax.ppermute(mine, "dom", [(i, i ^ 1) for i in range(STEPS)])
    density = jnp.sum(swap(grid, ("y", "hist")).astype(f32), axis=0).astype(bf16)
    fresh = to_all(density, ("dom", "hist"))

    partial, history_out = field_parts(
        place, fresh, mine, other, kernel_cols[:STEPS], rows_flat, mixed_old, kept, bands
    )
    received = swap(partial, ("y", "dom", "xh"))
    share = received.shape[1]
    by_column = jnp.sum(received.reshape(bands // 2, STEPS, 2, share, 2 * NG).astype(f32), axis=(0, 2))
    by_column = by_column.reshape(hist_size, -1, 2 * NG)
    summed = jnp.sum(swap(by_column, "hist"), axis=0).astype(bf16)
    field = to_all(summed, ("y", "hist")).reshape(NG // 2, 2 * NG)

    kick = swap(kicks(half, particles, field), ("dom", "xh"))
    kick_sum = jnp.sum(kick, axis=0).reshape(2, count)
    momentum_out = momentum + kick_scale * kick_sum

    return momentum_out, history_out


def solution(mesh):
    split = {"hist": ("hist",), "rows": ("xh", "y"), "dom": ("dom",)}
    sizes = [mesh.shape["hist"], 2, mesh.shape["rows"] // 2, mesh.shape["dom"]]
    fine = jax.sharding.Mesh(mesh.devices.reshape(sizes), ("hist", "xh", "y", "dom"))

    def spec(*dims):
        return P(*[None if dim is None else tuple(a for name in dim for a in split[name]) for dim in dims])

    everyone = ("hist", "rows", "dom")
    in_specs = (
        spec(None, everyone),
        spec(None, everyone),
        spec(None, everyone),
        spec(everyone),
        spec(None, everyone),
        spec(["hist"], ["rows"], None),
        spec(["hist"], ["dom"], None),
        spec(["hist"], ["rows"], None, None),
    )
    out_specs = (spec(None, everyone), spec(["hist"], ["rows"], None))
    return jax.shard_map(local, mesh=fine, in_specs=in_specs, out_specs=out_specs, check_vma=False)
```

```python
import functools

import jax
import jax.numpy as jnp
from jax import lax
from jax.experimental import pallas as pl
from jax.experimental.pallas import tpu as pltpu
from jax.sharding import PartitionSpec as P

NG = 512
BINS = 16
STEPS = 4
LANES = 128

kick_scale = 0.5
f32 = jnp.float32
bf16 = jnp.bfloat16


def swap(array, axes):
    return lax.all_to_all(array, axes, split_axis=0, concat_axis=0, tiled=True)


def to_all(array, axes):
    copies = jnp.broadcast_to(array, (lax.axis_size(axes), *array.shape))
    return swap(copies, axes)


def hat(places, cell, fraction):
    return jnp.maximum(1.0 - jnp.abs((places - cell) - fraction), jnp.zeros((), bf16))


def window(cell, first):
    return jnp.clip(cell - first, -2.0, 258.0).astype(bf16)


def unpack(particles, source):
    def field(which):
        return particles[source, which : which + 1, :]

    bins = field(2)
    row_bin = jnp.floor(bins * (1.0 / BINS))
    col_bin = bins - row_bin * BINS
    row_fraction = ((row_bin + 0.5) * (1.0 / BINS)).astype(bf16)
    col_fraction = ((col_bin + 0.5) * (1.0 / BINS)).astype(bf16)
    return field(0), row_fraction, field(1), col_fraction, field(3)


def lines_of(count, size):
    return lax.broadcasted_iota(jnp.int32, (count, size), 0)


def pack_kernel(core, row, col, bins, charge, history, out, tail, sem):
    count_out = tail.shape[0]
    first = history.shape[0] - STEPS + count_out * core[0]
    fetch = pltpu.make_async_copy(history.at[pl.ds(first, count_out)], tail, sem)
    fetch.start()
    steps, count = row.shape
    weight = charge[...].astype(f32).reshape(1, count)
    halves = out.shape[0] // steps
    for step in range(steps):
        fields = [ref[step : step + 1, :].astype(f32) for ref in (row, col, bins)]
        packed = jnp.concatenate(fields + [weight], axis=0)
        for half in range(halves):
            out[step * halves + half] = packed
    fetch.wait()


def pack(core, row, col, bins, charge, history, halves):
    steps, count = row.shape
    vmem = pl.BlockSpec(memory_space=pltpu.VMEM)
    return pl.pallas_call(
        pack_kernel,
        in_specs=[pl.BlockSpec(memory_space=pltpu.SMEM)] + [vmem] * 4 + [pl.BlockSpec(memory_space=pl.ANY)],
        out_specs=(vmem, pl.BlockSpec(memory_space=pl.ANY)),
        out_shape=(
            jax.ShapeDtypeStruct((halves * steps, 4, count), f32),
            jax.ShapeDtypeStruct((2, *history.shape[1:]), bf16),
        ),
        scratch_shapes=[pltpu.SemaphoreType.DMA],
        name="pack",
    )(core, row, col, bins, charge, history)


def deposit_kernel(lines, band, parts, half, particles, out):
    sources, _, count = particles.shape
    bands, share = lines // band, band // parts
    places = lines_of(lines, count).astype(f32).astype(bf16)
    total = None
    for source in range(sources):
        row, row_fraction, col, col_fraction, charge = unpack(particles, source)
        row_table = hat(places, window(row, (half[0] * lines).astype(f32)), row_fraction) * charge.astype(bf16)
        col_tables = [hat(places, window(col, float(first)), col_fraction) for first in range(0, NG, lines)]
        col_table = jnp.concatenate(col_tables, axis=0)
        part = lax.dot_general(row_table, col_table, (((1,), (1,)), ((), ())), preferred_element_type=f32)
        total = part if total is None else total + part
    grid = total.astype(bf16)
    for n in range(bands * parts):
        at, part = divmod(n, parts)
        first = at * band + part * share
        out[n] = grid[first : first + share]


def deposit(half, particles, lines, band, parts):
    blocks = (lines // band * parts, band // parts, NG)
    vmem = pl.BlockSpec(memory_space=pltpu.VMEM)
    return pl.pallas_call(
        functools.partial(deposit_kernel, lines, band, parts),
        in_specs=[pl.BlockSpec(memory_space=pltpu.SMEM), vmem],
        out_specs=vmem,
        out_shape=jax.ShapeDtypeStruct(blocks, bf16),
        compiler_params=pltpu.CompilerParams(vmem_limit_bytes=48 << 20),
        cost_estimate=pl.CostEstimate(flops=4 * NG * NG * 4096, transcendentals=0, bytes_accessed=1 << 20),
        name="deposit",
    )(half, particles)


def kick_kernel(half, particles, field, out):
    sources, _, count = particles.shape
    width = field.shape[0]
    lines = count // LANES
    places = lines_of(width, count)
    row_places = places.astype(f32).astype(bf16)
    column = ((places >> 4) & 3) * 128 + (places >> 6) * 16 + (places & 15)
    column = column.astype(f32)

    def tables(source):
        row, row_fraction, col, col_fraction, _ = unpack(particles, source)
        row_tables = [hat(row_places, window(row, float(first)), row_fraction) for first in range(0, NG, width)]
        at_col = col + col_fraction.astype(f32) - (half[0] * 64).astype(f32)
        return jnp.concatenate(row_tables, axis=0), jnp.maximum(1.0 - jnp.abs(column - at_col), 0.0)

    ready = tables(0)
    for source in range(sources):
        row_table, col_table = ready
        if source + 1 < sources:
            ready = tables(source + 1)
        for comp in range(2):
            along = jnp.dot(field[:, comp * NG : (comp + 1) * NG], row_table, preferred_element_type=f32)
            kick = jnp.sum(along * col_table, axis=0, keepdims=True)
            for k in range(lines):
                out[source, comp * lines + k : comp * lines + k + 1, :] = kick[:, k * LANES : (k + 1) * LANES]


def kicks(half, particles, field):
    sources, _, count = particles.shape
    vmem = pl.BlockSpec(memory_space=pltpu.VMEM)
    return pl.pallas_call(
        kick_kernel,
        in_specs=[pl.BlockSpec(memory_space=pltpu.SMEM), vmem, vmem],
        out_specs=vmem,
        out_shape=jax.ShapeDtypeStruct((sources, 2 * count // LANES, LANES), f32),
        compiler_params=pltpu.CompilerParams(vmem_limit_bytes=48 << 20),
        name="kicks",
    )(half, particles, field)


def old_mixed_kernel(history, cols, out, kept):
    lags, band, _ = history.shape
    for lag in range(1, lags):
        steps = min(lag, STEPS)
        grids = history[lag - steps : lag].reshape(steps * band, NG)
        mixed = lax.dot_general(grids, cols[lag], (((1,), (1,)), ((), ())), preferred_element_type=f32)
        mixed = mixed.astype(bf16).reshape(steps, band, mixed.shape[1])
        for step in range(steps):
            out[step, lag] = mixed[steps - 1 - step]
    for step in range(STEPS):
        for lag in range(step + 1):
            out[step, lag] = jnp.zeros(out.shape[2:], bf16)
    kept[STEPS:] = history[: lags - STEPS]


def old_mixed(history, cols):
    lags, band, _ = history.shape
    return pl.pallas_call(
        old_mixed_kernel,
        out_shape=(
            jax.ShapeDtypeStruct((STEPS, lags, band, cols.shape[1]), bf16),
            jax.ShapeDtypeStruct(history.shape, bf16),
        ),
        compiler_params=pltpu.CompilerParams(vmem_limit_bytes=48 << 20),
        name="old_mixed",
    )(history, cols)


def field_kernel(first, core, fresh, mine, other, cols, rows, mixed_old, kept, out, cycle, newer, sem):
    band = mine.shape[1]
    parts_in = fresh.shape[0] // STEPS
    ahead = []
    for n in range(STEPS):
        density = [fresh[(STEPS - 1 - n) * parts_in + part] for part in range(parts_in)]
        older = jnp.where(core[0] == n // 2, mine[n % 2], other[n % 2])
        ahead.append(jnp.where(first[0] == 1, jnp.concatenate(density, axis=0), older))
        newer[n] = ahead[n]
    store = pltpu.make_async_copy(newer, cycle.at[pl.ds(0, STEPS)], sem)
    store.start()
    grids = jnp.concatenate(ahead, axis=0)
    wide = cols.shape[1]
    parts = [[] for _ in range(STEPS)]
    for lag in range(STEPS):
        count = STEPS - lag
        mixed = lax.dot_general(
            grids[lag * band :], cols[lag], (((1,), (1,)), ((), ())), preferred_element_type=f32
        ).astype(bf16)
        for n in range(count):
            parts[STEPS - 1 - n].append(mixed[n * band : (n + 1) * band])
    bands = out.shape[0] // STEPS
    share = wide // bands
    for step in range(STEPS):
        lines = parts[step] + [mixed_old[step, lag] for lag in range(step + 1, mixed_old.shape[1])]
        lhs = jnp.concatenate(lines, axis=0)
        field = lax.dot_general(lhs, rows[...], (((0,), (0,)), ((), ())), preferred_element_type=f32)
        field = field.astype(bf16)
        for band_to in range(bands):
            half, quarter = divmod(band_to, bands // 2)
            out[(quarter * STEPS + step) * 2 + half] = field[band_to * share : (band_to + 1) * share]
    store.wait()


def field_parts(place, fresh, mine, other, cols, rows, mixed_old, kept, bands):
    wide = cols.shape[1]
    vmem = pl.BlockSpec(memory_space=pltpu.VMEM)
    return pl.pallas_call(
        field_kernel,
        in_specs=[pl.BlockSpec(memory_space=pltpu.SMEM)] * 2 + [vmem] * 6 + [pl.BlockSpec(memory_space=pl.ANY)],
        out_specs=(vmem, pl.BlockSpec(memory_space=pl.ANY)),
        out_shape=(
            jax.ShapeDtypeStruct((bands * STEPS, wide // bands, rows.shape[1]), bf16),
            jax.ShapeDtypeStruct(kept.shape, bf16),
        ),
        scratch_shapes=[pltpu.VMEM((STEPS, *mine.shape[1:]), bf16), pltpu.SemaphoreType.DMA],
        input_output_aliases={8: 1},
        compiler_params=pltpu.CompilerParams(vmem_limit_bytes=48 << 20),
        name="field_parts",
    )(*place, fresh, mine, other, cols, rows, mixed_old, kept)


def local(row_index, col_index, bin_index, charge, momentum, history, kernel_cols, kernel_rows):
    lags, band, _ = history.shape
    count = charge.shape[0]
    bands = NG // band
    hist_at = lax.axis_index("hist")
    hist_size = lax.axis_size("hist")

    core = lax.axis_index("dom") % 2
    packed, tail = pack(core.reshape(1), row_index, col_index, bin_index, charge, history, 2)
    particles = swap(packed, ("dom", "xh"))
    half = lax.axis_index("xh").reshape(1)
    place = [(hist_at == 0).astype(jnp.int32).reshape(1), core.reshape(1)]

    mixed_old, kept = old_mixed(history, kernel_cols)
    mine = lax.ppermute(tail, "hist", [(i, i + 1) for i in range(hist_size - 1)])
    rows_flat = kernel_rows.reshape(lags * band, 2 * NG)

    grid = deposit(half, particles, NG // 2, band, hist_size)
    grid, mine = lax.optimization_barrier((grid, mine))
    other = lax.ppermute(mine, "dom", [(i, i ^ 1) for i in range(STEPS)])
    density = jnp.sum(swap(grid, ("y", "hist")).astype(f32), axis=0).astype(bf16)
    fresh = to_all(density, ("dom", "hist"))

    partial, history_out = field_parts(
        place, fresh, mine, other, kernel_cols[:STEPS], rows_flat, mixed_old, kept, bands
    )
    received = swap(partial, ("y", "dom", "xh"))
    share = received.shape[1]
    by_column = jnp.sum(received.reshape(bands // 2, STEPS, 2, share, 2 * NG).astype(f32), axis=(0, 2))
    by_column = by_column.reshape(hist_size, -1, 2 * NG)
    summed = jnp.sum(swap(by_column, "hist"), axis=0).astype(bf16)
    field = to_all(summed, ("y", "hist")).reshape(NG // 2, 2 * NG)

    kick = swap(kicks(half, particles, field), ("dom", "xh"))
    kick_sum = jnp.sum(kick, axis=0).reshape(2, count)
    momentum_out = momentum + kick_scale * kick_sum

    return momentum_out, history_out


def solution(mesh):
    split = {"hist": ("hist",), "rows": ("xh", "y"), "dom": ("dom",)}
    sizes = [mesh.shape["hist"], 2, mesh.shape["rows"] // 2, mesh.shape["dom"]]
    fine = jax.sharding.Mesh(mesh.devices.reshape(sizes), ("hist", "xh", "y", "dom"))

    def spec(*dims):
        return P(*[None if dim is None else tuple(a for name in dim for a in split[name]) for dim in dims])

    everyone = ("hist", "rows", "dom")
    in_specs = (
        spec(None, everyone),
        spec(None, everyone),
        spec(None, everyone),
        spec(everyone),
        spec(None, everyone),
        spec(["hist"], ["rows"], None),
        spec(["hist"], ["dom"], None),
        spec(["hist"], ["rows"], None, None),
    )
    out_specs = (spec(None, everyone), spec(["hist"], ["rows"], None))
    return jax.shard_map(local, mesh=fine, in_specs=in_specs, out_specs=out_specs, check_vma=False)
```

```python
import functools

import jax
import jax.numpy as jnp
from jax import lax
from jax.experimental import pallas as pl
from jax.experimental.pallas import tpu as pltpu
from jax.sharding import PartitionSpec as P

NG = 512
BINS = 16
STEPS = 4
LANES = 128

kick_scale = 0.5
f32 = jnp.float32
bf16 = jnp.bfloat16


def swap(array, axes):
    return lax.all_to_all(array, axes, split_axis=0, concat_axis=0, tiled=True)


def to_all(array, axes):
    copies = jnp.broadcast_to(array, (lax.axis_size(axes), *array.shape))
    return swap(copies, axes)


def hat(places, cell, fraction):
    return jnp.maximum(1.0 - jnp.abs((places - cell) - fraction), jnp.zeros((), bf16))


def window(cell, first):
    return jnp.clip(cell - first, -2.0, 258.0).astype(bf16)


def unpack(particles, source):
    def field(which):
        return particles[source, which : which + 1, :]

    bins = field(2)
    row_bin = jnp.floor(bins * (1.0 / BINS))
    col_bin = bins - row_bin * BINS
    row_fraction = ((row_bin + 0.5) * (1.0 / BINS)).astype(bf16)
    col_fraction = ((col_bin + 0.5) * (1.0 / BINS)).astype(bf16)
    return field(0), row_fraction, field(1), col_fraction, field(3)


def lines_of(count, size):
    return lax.broadcasted_iota(jnp.int32, (count, size), 0)


def pack_kernel(core, row, col, bins, charge, history, out, tail, sem):
    count_out = tail.shape[0]
    first = history.shape[0] - STEPS + count_out * core[0]
    fetch = pltpu.make_async_copy(history.at[pl.ds(first, count_out)], tail, sem)
    fetch.start()
    steps, count = row.shape
    weight = charge[...].astype(f32).reshape(1, count)
    halves = out.shape[0] // steps
    for step in range(steps):
        fields = [ref[step : step + 1, :].astype(f32) for ref in (row, col, bins)]
        packed = jnp.concatenate(fields + [weight], axis=0)
        for half in range(halves):
            out[step * halves + half] = packed
    fetch.wait()


def pack(core, row, col, bins, charge, history, halves):
    steps, count = row.shape
    vmem = pl.BlockSpec(memory_space=pltpu.VMEM)
    return pl.pallas_call(
        pack_kernel,
        in_specs=[pl.BlockSpec(memory_space=pltpu.SMEM)] + [vmem] * 4 + [pl.BlockSpec(memory_space=pl.ANY)],
        out_specs=(vmem, vmem),
        out_shape=(
            jax.ShapeDtypeStruct((halves * steps, 4, count), f32),
            jax.ShapeDtypeStruct((2, *history.shape[1:]), bf16),
        ),
        scratch_shapes=[pltpu.SemaphoreType.DMA],
        name="pack",
    )(core, row, col, bins, charge, history)


def deposit_kernel(lines, band, parts, half, particles, out):
    sources, _, count = particles.shape
    bands, share = lines // band, band // parts
    places = lines_of(lines, count).astype(f32).astype(bf16)
    total = None
    for source in range(sources):
        row, row_fraction, col, col_fraction, charge = unpack(particles, source)
        row_table = hat(places, window(row, (half[0] * lines).astype(f32)), row_fraction) * charge.astype(bf16)
        col_tables = [hat(places, window(col, float(first)), col_fraction) for first in range(0, NG, lines)]
        col_table = jnp.concatenate(col_tables, axis=0)
        part = lax.dot_general(row_table, col_table, (((1,), (1,)), ((), ())), preferred_element_type=f32)
        total = part if total is None else total + part
    grid = total.astype(bf16)
    for n in range(bands * parts):
        at, part = divmod(n, parts)
        first = at * band + part * share
        out[n] = grid[first : first + share]


def deposit(half, particles, lines, band, parts):
    blocks = (lines // band * parts, band // parts, NG)
    vmem = pl.BlockSpec(memory_space=pltpu.VMEM)
    return pl.pallas_call(
        functools.partial(deposit_kernel, lines, band, parts),
        in_specs=[pl.BlockSpec(memory_space=pltpu.SMEM), vmem],
        out_specs=vmem,
        out_shape=jax.ShapeDtypeStruct(blocks, bf16),
        compiler_params=pltpu.CompilerParams(vmem_limit_bytes=48 << 20),
        cost_estimate=pl.CostEstimate(flops=4 * NG * NG * 4096, transcendentals=0, bytes_accessed=1 << 20),
        name="deposit",
    )(half, particles)


def kick_kernel(half, particles, field, out):
    sources, _, count = particles.shape
    width = field.shape[0]
    lines = count // LANES
    places = lines_of(width, count)
    row_places = places.astype(f32).astype(bf16)
    column = ((places >> 4) & 3) * 128 + (places >> 6) * 16 + (places & 15)
    column = column.astype(f32)

    def tables(source):
        row, row_fraction, col, col_fraction, _ = unpack(particles, source)
        row_tables = [hat(row_places, window(row, float(first)), row_fraction) for first in range(0, NG, width)]
        at_col = col + col_fraction.astype(f32) - (half[0] * 64).astype(f32)
        return jnp.concatenate(row_tables, axis=0), jnp.maximum(1.0 - jnp.abs(column - at_col), 0.0)

    ready = tables(0)
    for source in range(sources):
        row_table, col_table = ready
        if source + 1 < sources:
            ready = tables(source + 1)
        for comp in range(2):
            along = jnp.dot(field[:, comp * NG : (comp + 1) * NG], row_table, preferred_element_type=f32)
            kick = jnp.sum(along * col_table, axis=0, keepdims=True)
            for k in range(lines):
                out[source, comp * lines + k : comp * lines + k + 1, :] = kick[:, k * LANES : (k + 1) * LANES]


def kicks(half, particles, field):
    sources, _, count = particles.shape
    vmem = pl.BlockSpec(memory_space=pltpu.VMEM)
    return pl.pallas_call(
        kick_kernel,
        in_specs=[pl.BlockSpec(memory_space=pltpu.SMEM), vmem, vmem],
        out_specs=vmem,
        out_shape=jax.ShapeDtypeStruct((sources, 2 * count // LANES, LANES), f32),
        compiler_params=pltpu.CompilerParams(vmem_limit_bytes=48 << 20),
        name="kicks",
    )(half, particles, field)


def old_mixed_kernel(history, cols, out, kept):
    lags, band, _ = history.shape
    for lag in range(1, lags):
        steps = min(lag, STEPS)
        grids = history[lag - steps : lag].reshape(steps * band, NG)
        mixed = lax.dot_general(grids, cols[lag], (((1,), (1,)), ((), ())), preferred_element_type=f32)
        mixed = mixed.astype(bf16).reshape(steps, band, mixed.shape[1])
        for step in range(steps):
            out[step, lag] = mixed[steps - 1 - step]
    for step in range(STEPS):
        for lag in range(step + 1):
            out[step, lag] = jnp.zeros(out.shape[2:], bf16)
    kept[STEPS:] = history[: lags - STEPS]


def old_mixed(history, cols):
    lags, band, _ = history.shape
    return pl.pallas_call(
        old_mixed_kernel,
        out_shape=(
            jax.ShapeDtypeStruct((STEPS, lags, band, cols.shape[1]), bf16),
            jax.ShapeDtypeStruct(history.shape, bf16),
        ),
        compiler_params=pltpu.CompilerParams(vmem_limit_bytes=48 << 20),
        name="old_mixed",
    )(history, cols)


def field_kernel(first, core, fresh, mine, other, cols, rows, mixed_old, kept, out, cycle, newer, sem):
    band = mine.shape[1]
    parts_in = fresh.shape[0] // STEPS
    ahead = []
    for n in range(STEPS):
        density = [fresh[(STEPS - 1 - n) * parts_in + part] for part in range(parts_in)]
        older = jnp.where(core[0] == n // 2, mine[n % 2], other[n % 2])
        ahead.append(jnp.where(first[0] == 1, jnp.concatenate(density, axis=0), older))
        newer[n] = ahead[n]
    store = pltpu.make_async_copy(newer, cycle.at[pl.ds(0, STEPS)], sem)
    store.start()
    grids = jnp.concatenate(ahead, axis=0)
    wide = cols.shape[1]
    parts = [[] for _ in range(STEPS)]
    for lag in range(STEPS):
        count = STEPS - lag
        mixed = lax.dot_general(
            grids[lag * band :], cols[lag], (((1,), (1,)), ((), ())), preferred_element_type=f32
        ).astype(bf16)
        for n in range(count):
            parts[STEPS - 1 - n].append(mixed[n * band : (n + 1) * band])
    bands = out.shape[0] // STEPS
    share = wide // bands
    for step in range(STEPS):
        lines = parts[step] + [mixed_old[step, lag] for lag in range(step + 1, mixed_old.shape[1])]
        lhs = jnp.concatenate(lines, axis=0)
        field = lax.dot_general(lhs, rows[...], (((0,), (0,)), ((), ())), preferred_element_type=f32)
        field = field.astype(bf16)
        for band_to in range(bands):
            half, quarter = divmod(band_to, bands // 2)
            out[(quarter * STEPS + step) * 2 + half] = field[band_to * share : (band_to + 1) * share]
    store.wait()


def field_parts(place, fresh, mine, other, cols, rows, mixed_old, kept, bands):
    wide = cols.shape[1]
    vmem = pl.BlockSpec(memory_space=pltpu.VMEM)
    return pl.pallas_call(
        field_kernel,
        in_specs=[pl.BlockSpec(memory_space=pltpu.SMEM)] * 2 + [vmem] * 6 + [pl.BlockSpec(memory_space=pl.ANY)],
        out_specs=(vmem, pl.BlockSpec(memory_space=pl.ANY)),
        out_shape=(
            jax.ShapeDtypeStruct((bands * STEPS, wide // bands, rows.shape[1]), bf16),
            jax.ShapeDtypeStruct(kept.shape, bf16),
        ),
        scratch_shapes=[pltpu.VMEM((STEPS, *mine.shape[1:]), bf16), pltpu.SemaphoreType.DMA],
        input_output_aliases={8: 1},
        compiler_params=pltpu.CompilerParams(vmem_limit_bytes=48 << 20),
        name="field_parts",
    )(*place, fresh, mine, other, cols, rows, mixed_old, kept)


def local(row_index, col_index, bin_index, charge, momentum, history, kernel_cols, kernel_rows):
    lags, band, _ = history.shape
    count = charge.shape[0]
    bands = NG // band
    hist_at = lax.axis_index("hist")
    hist_size = lax.axis_size("hist")

    core = lax.axis_index("dom") % 2
    packed, tail = pack(core.reshape(1), row_index, col_index, bin_index, charge, history, 2)
    particles = swap(packed, ("dom", "xh"))
    half = lax.axis_index("xh").reshape(1)
    place = [(hist_at == 0).astype(jnp.int32).reshape(1), core.reshape(1)]

    mixed_old, kept = old_mixed(history, kernel_cols)
    mine = lax.ppermute(tail, "hist", [(i, i + 1) for i in range(hist_size - 1)])
    rows_flat = kernel_rows.reshape(lags * band, 2 * NG)

    grid = deposit(half, particles, NG // 2, band, hist_size)
    grid, mine = lax.optimization_barrier((grid, mine))
    other = lax.ppermute(mine, "dom", [(i, i ^ 1) for i in range(STEPS)])
    density = jnp.sum(swap(grid, ("y", "hist")).astype(f32), axis=0).astype(bf16)
    fresh = to_all(density, ("dom", "hist"))

    partial, history_out = field_parts(
        place, fresh, mine, other, kernel_cols[:STEPS], rows_flat, mixed_old, kept, bands
    )
    received = swap(partial, ("y", "dom", "xh"))
    share = received.shape[1]
    by_column = jnp.sum(received.reshape(bands // 2, STEPS, 2, share, 2 * NG).astype(f32), axis=(0, 2))
    by_column = by_column.reshape(hist_size, -1, 2 * NG)
    summed = jnp.sum(swap(by_column, "hist"), axis=0).astype(bf16)
    field = to_all(summed, ("y", "hist")).reshape(NG // 2, 2 * NG)

    kick = swap(kicks(half, particles, field), ("dom", "xh"))
    kick_sum = jnp.sum(kick, axis=0).reshape(2, count)
    momentum_out = momentum + kick_scale * kick_sum

    return momentum_out, history_out


def solution(mesh):
    split = {"hist": ("hist",), "rows": ("xh", "y"), "dom": ("dom",)}
    sizes = [mesh.shape["hist"], 2, mesh.shape["rows"] // 2, mesh.shape["dom"]]
    fine = jax.sharding.Mesh(mesh.devices.reshape(sizes), ("hist", "xh", "y", "dom"))

    def spec(*dims):
        return P(*[None if dim is None else tuple(a for name in dim for a in split[name]) for dim in dims])

    everyone = ("hist", "rows", "dom")
    in_specs = (
        spec(None, everyone),
        spec(None, everyone),
        spec(None, everyone),
        spec(everyone),
        spec(None, everyone),
        spec(["hist"], ["rows"], None),
        spec(["hist"], ["dom"], None),
        spec(["hist"], ["rows"], None, None),
    )
    out_specs = (spec(None, everyone), spec(["hist"], ["rows"], None))
    return jax.shard_map(local, mesh=fine, in_specs=in_specs, out_specs=out_specs, check_vma=False)
```
